32 devices in a mesh: tile: 8 (over y, x, core), trac: 4 (over z).
Axes of the slice: x: 2, y: 2, z: 4, core: 2. Of those that a mesh axis runs over, the one named last changes fastest.
Arguments:
- tracers: float32 [128, 512, 128], P(None, ('tile', 'trac')), may hold values from -6 to 6
- winds: float32 [2, 512, 128], P(None, ('tile', 'trac')), may hold values from -4 to 4
- chem_linear: float32 [128, 128], replicated, may hold values from -0.5 to 0.5
- chem_loss: float32 [128], replicated, may hold values from 0.5 to 4
- chem_left: float32 [4, 128, 128], replicated, may hold values from -0.25 to 0.25
- chem_right: float32 [4, 128, 128], replicated, may hold values from -0.25 to 0.25
- active_cells: int32 [32], P(('tile', 'trac')), may hold values from 256 to 2048
Outputs:
- tracers_out: float32 [128, 512, 128], P(None, ('tile', 'trac'))
- winds_out: float32 [2, 512, 128], P(None, ('tile', 'trac'))
The draws below stay inside these ranges and needn't reach their ends.
Inputs may be any that keep to these rules, and one draw needn't show every extreme that they name: `active_cells`: active cells are the leading ones of the tile in row-major order.
All inputs are finite; a program needn't handle non-finite values.
Results may differ from the reference program's by a relative error of at most 0.0003.
Values sent between devices are 32-bit elements; how exact they have to be, the bound alone decides.
A program may use at most 64 MiB of HBM per device.

```python
import math
from functools import partial
import jax
import jax.numpy as jnp
from jax import lax

SPECIES = 128
W = 128
SUBS = 4
CHEM_STEPS = 3
PAIRS = 4
TILES = 32
ROWS = 512
CELLS = 2048


def with_ends(result, rng, smallest, largest):
    extent = result.shape
    spot = [jax.random.randint(jax.random.fold_in(rng, axis), (), 0, extent[axis]) for axis in range(len(extent))]
    result = result.at[tuple(spot)].set(smallest)
    longest = extent.index(max(extent))
    spot[longest] = (spot[longest] + 1) % extent[longest]
    return result.at[tuple(spot)].set(largest)


def levels(own_key, extent, shards, smallest, top_value):
    gain, own = 1.0, jax.random.fold_in(own_key, 6)
    for position, shards_of in shards:
        heights = jnp.exp(jax.random.uniform(jax.random.fold_in(own, position), (shards_of,), jnp.float32, smallest / len(shards), top_value / len(shards)))
        gain = gain * jnp.repeat(heights, extent[position] // shards_of).reshape([-1 if axis == position else 1 for axis in range(len(extent))])
    return gain


def scatter_about(key, dims, scale, reach, pieces=(), kind=jnp.bfloat16):
    entries = jax.random.normal(key, dims, jnp.float32) * scale
    if len(pieces) > 0:
        entries = levels(key, dims, pieces, -0.22, 0.18) * entries
    return jnp.clip(entries, min=-reach, max=reach).astype(kind)


def setup_inputs(seed: int = 0) -> dict:
    seeds = jax.random.split(jax.random.key(seed), 8)
    return {
        "tracers": scatter_about(seeds[0], (SPECIES, ROWS, W), 1.0, 6.0, ((1, 32),), jnp.float32),
        "winds": scatter_about(seeds[1], (2, ROWS, W), 1.0, 4.0, ((1, 32),), jnp.float32),
        "chem_linear": scatter_about(seeds[2], (SPECIES, SPECIES), SPECIES ** -0.5, 0.5, (), jnp.float32),
        "chem_loss": jnp.clip(jnp.exp(jax.random.uniform(seeds[3], (SPECIES,), jnp.float32, math.log(0.5), math.log(4.0))), 0.5, 4.0),
        "chem_left": scatter_about(seeds[4], (PAIRS, SPECIES, SPECIES), (4 * SPECIES) ** -0.5, 0.25, (), jnp.float32),
        "chem_right": scatter_about(seeds[5], (PAIRS, SPECIES, SPECIES), (4 * SPECIES) ** -0.5, 0.25, (), jnp.float32),
        "active_cells": with_ends(jax.random.randint(seeds[6], (TILES,), CELLS // 8, CELLS + 1), jax.random.fold_in(seeds[6], 1), CELLS // 8, CELLS).astype(jnp.int32),
    }


DT_WIND = 0.1
VISCOSITY = 0.2
DT_TRACER = 0.1
DT_CHEM = 0.1


def wrap_rows(field, width):
    return jnp.concatenate([field[:, field.shape[1] - width:, :], field, field[:, :width, :]], axis=1)


def tendency(extended):
    centre = extended[:, 1:-1, :]
    along = (jnp.roll(centre, -1, axis=2) - jnp.roll(centre, 1, axis=2)) * 0.5
    across = (extended[:, 2:, :] - extended[:, :-2, :]) * 0.5
    spread = jnp.roll(centre, -1, axis=2) + jnp.roll(centre, 1, axis=2) + extended[:, 2:, :] + extended[:, :-2, :] - 4.0 * centre
    return -(centre[0:1] * along + centre[1:2] * across) + VISCOSITY * spread


def wind_step(winds, rim):
    first = winds + DT_WIND * tendency(rim(winds))
    second = 0.75 * winds + 0.25 * (first + DT_WIND * tendency(rim(first)))
    return winds / 3.0 + 2.0 / 3.0 * (second + DT_WIND * tendency(rim(second)))


def advect(extended):
    tracer = extended[:-2]
    east = extended[-2, 1:-1, :]
    north = extended[-1]
    centre = tracer[:, 1:-1, :]
    flux = jnp.maximum(east, 0.0) * centre + jnp.minimum(jnp.roll(east, -1, axis=1), 0.0) * jnp.roll(centre, -1, axis=2)
    div_x = flux - jnp.roll(flux, 1, axis=2)
    upward = jnp.maximum(north[:-1], 0.0) * tracer[:, :-1, :] + jnp.minimum(north[1:], 0.0) * tracer[:, 1:, :]
    div_y = upward[:, 1:, :] - upward[:, :-1, :]
    moved = centre - DT_TRACER * (div_x + div_y)
    return jnp.concatenate([moved, extended[-2:, 1:-1, :]], axis=0)


def react(conc, active, linear, loss, both_factors):
    species = conc.shape[0]
    for step in range(CHEM_STEPS):
        rate = jnp.dot(linear, conc, precision=lax.Precision.HIGHEST, preferred_element_type=jnp.float32) - loss[:, None] * conc
        factors = jnp.dot(both_factors, conc, precision=lax.Precision.HIGHEST, preferred_element_type=jnp.float32)
        factors = factors.reshape(2, PAIRS, species, conc.shape[1])
        rate = rate + jnp.sum(factors[0] * factors[1], axis=0)
        conc = conc + DT_CHEM * (rate * active[None, :])
    return conc


def reference(tracers, winds, chem_linear, chem_loss, chem_left, chem_right, active_cells):
    rim = partial(wrap_rows, width=1)
    winds_new = wind_step(winds, rim)
    stretch = math.gcd(SPECIES, 8)
    grouped = tracers.reshape(SPECIES // stretch, stretch, ROWS, W)

    def carry_block(block):
        state = jnp.concatenate([block, winds_new], axis=0)
        for sub in range(SUBS):
            state = advect(rim(state))
        return state[:-2]

    moved = lax.map(carry_block, grouped).reshape(SPECIES, ROWS, W)
    tiled = moved.reshape(SPECIES, TILES, CELLS).transpose(1, 0, 2)
    both_factors = jnp.concatenate([chem_left, chem_right], axis=0).reshape(2 * PAIRS * SPECIES, SPECIES)

    def chem_tile(item):
        conc, count = item
        mask = (jnp.arange(CELLS, dtype=jnp.int32) < count).astype(jnp.float32)
        return react(conc, mask, chem_linear, chem_loss, both_factors)

    done = lax.map(chem_tile, (tiled, active_cells))
    return done.transpose(1, 0, 2).reshape(SPECIES, ROWS, W), winds_new
```

```python
import functools

import jax
import jax.numpy as jnp
from jax import lax
from jax.experimental import pallas as pl
from jax.experimental.pallas import tpu as pltpu
from jax.sharding import PartitionSpec as P

SUBS = 4
CHEM_STEPS = 3
WIND_STAGES = 3

DT_WIND = 0.1
VISCOSITY = 0.2
DT_TRACER = 0.1
DT_CHEM = 0.1

AXES = ("tile", "trac")
MESH = pl.DeviceIdType.MESH


def kernel(
    sizes,
    count_ref,
    tracers,
    winds,
    linear,
    loss,
    left,
    right,
    tracers_out,
    winds_out,
    lev,
    wind,
    wind_new,
    coef,
    lin_v,
    loss_v,
    fac_v,
    weights,
    done,
    row_sem,
    par_sem,
    wind_sem,
    out_sem,
    wout_sem,
    send_sem,
    recv_sem,
    wsend_sem,
    wrecv_sem,
):
    tiles, tracs = sizes
    species, rows, width = tracers.shape
    pairs = left.shape[0]
    depth = SUBS
    reach = SUBS + WIND_STAGES
    wrows = wind.shape[1]
    base = (wrows - rows) // 2
    shift = base - depth
    devices = tiles * tracs
    me = lax.axis_index(AXES[0]) * tracs + lax.axis_index(AXES[1])
    up_flat = lax.rem(me + 1, devices)
    down_flat = lax.rem(me + devices - 1, devices)
    up = (up_flat // tracs, lax.rem(up_flat, tracs))
    down = (down_flat // tracs, lax.rem(down_flat, tracs))

    barrier = pltpu.get_barrier_semaphore()
    for neighbour in (up, down):
        pl.semaphore_signal(barrier, inc=1, device_id=neighbour, device_id_type=MESH)

    order = []
    for k in range(depth):
        order += [rows - 1 - k, k]
    order += list(range(depth, rows - depth))

    def row_copy(r):
        return pltpu.make_async_copy(tracers.at[:, r, :], lev.at[0, depth + r], row_sem.at[r])

    own_wind = pltpu.make_async_copy(winds, wind.at[:, base : base + rows, :], wind_sem)
    own_wind.start()
    for r in order:
        row_copy(r).start()
    params = [
        pltpu.make_async_copy(linear, lin_v, par_sem.at[0]),
        pltpu.make_async_copy(loss, loss_v, par_sem.at[1]),
        pltpu.make_async_copy(left, fac_v.at[0], par_sem.at[2]),
        pltpu.make_async_copy(right, fac_v.at[1], par_sem.at[3]),
    ]
    for copy in params:
        copy.start()

    def wind_send(side):
        first = rows - reach if side == 0 else 0
        there = base - reach if side == 0 else base + rows
        return pltpu.make_async_remote_copy(
            src_ref=winds.at[:, first : first + reach, :],
            dst_ref=wind.at[:, there : there + reach, :],
            send_sem=wsend_sem.at[side],
            recv_sem=wrecv_sem.at[side],
            device_id=up if side == 0 else down,
            device_id_type=MESH,
        )

    def halo_send(side, k):
        here = depth + rows - 1 - k if side == 0 else depth + k
        there = depth - 1 - k if side == 0 else depth + rows + k
        return pltpu.make_async_remote_copy(
            src_ref=lev.at[0, here],
            dst_ref=lev.at[0, there],
            send_sem=send_sem.at[side, k],
            recv_sem=recv_sem.at[side, k],
            device_id=up if side == 0 else down,
            device_id_type=MESH,
        )

    pl.semaphore_wait(barrier, 2)
    for side in range(2):
        wind_send(side).start()
    for k in range(depth):
        row_copy(rows - 1 - k).wait()
        halo_send(0, k).start()
        row_copy(k).wait()
        halo_send(1, k).start()

    for copy in params:
        copy.wait()
    diag = lax.broadcasted_iota(jnp.int32, (species, species), 0) == lax.broadcasted_iota(
        jnp.int32, (species, species), 1
    )

    def put(slot, value):
        high = value.astype(jnp.bfloat16)
        low = (value - high.astype(jnp.float32)).astype(jnp.bfloat16)
        lines = pl.ds(slot * species, species)
        weights[lines, :species] = high
        weights[lines, species : 2 * species] = low

    put(0, DT_CHEM * (lin_v[...] - jnp.where(diag, loss_v[...], 0.0)))
    for p in range(pairs):
        put(1 + p, DT_CHEM * fac_v[0, p])
        put(1 + pairs + p, fac_v[1, p])

    for r in range(depth, rows - depth):
        row_copy(r).wait()
    own_wind.wait()
    for side in range(2):
        wind_send(side).wait()

    raw = wind[...]
    u0, v0 = raw[0], raw[1]

    def tendency(u, v):
        def of(f):
            east = pltpu.roll(f, width - 1, 1)
            west = pltpu.roll(f, 1, 1)
            north = pltpu.roll(f, wrows - 1, 0)
            south = pltpu.roll(f, 1, 0)
            along = (east - west) * 0.5
            across = (north - south) * 0.5
            spread = east + west + north + south - 4.0 * f
            return -(u * along + v * across) + VISCOSITY * spread

        return of(u), of(v)

    tu, tv = tendency(u0, v0)
    u1, v1 = u0 + DT_WIND * tu, v0 + DT_WIND * tv
    tu, tv = tendency(u1, v1)
    u2 = 0.75 * u0 + 0.25 * (u1 + DT_WIND * tu)
    v2 = 0.75 * v0 + 0.25 * (v1 + DT_WIND * tv)
    tu, tv = tendency(u2, v2)
    u3 = u0 / 3.0 + 2.0 / 3.0 * (u2 + DT_WIND * tu)
    v3 = v0 / 3.0 + 2.0 / 3.0 * (v2 + DT_WIND * tv)
    wind_new[0] = u3[base : base + rows]
    wind_new[1] = v3[base : base + rows]
    wind_copy = pltpu.make_async_copy(wind_new, winds_out, wout_sem)
    wind_copy.start()

    coef[0] = 1.0 - DT_TRACER * (jnp.abs(u3) + jnp.abs(v3))
    coef[1] = pltpu.roll(DT_TRACER * jnp.maximum(u3, 0.0), 1, 1)
    coef[2] = pltpu.roll(-DT_TRACER * jnp.minimum(u3, 0.0), width - 1, 1)
    coef[3] = pltpu.roll(DT_TRACER * jnp.maximum(v3, 0.0), 1, 0)
    coef[4] = pltpu.roll(-DT_TRACER * jnp.minimum(v3, 0.0), wrows - 1, 0)

    def advance(level, i):
        line = pl.ds(i + shift, 1)
        q = lev[level - 1, i]
        moved = coef[0, line, :] * q
        moved += coef[1, line, :] * pltpu.roll(q, 1, 1)
        moved += coef[2, line, :] * pltpu.roll(q, width - 1, 1)
        moved += coef[3, line, :] * lev[level - 1, i - 1]
        moved += coef[4, line, :] * lev[level - 1, i + 1]
        lev[level, i] = moved

    for level in range(1, depth + 1):

        @pl.loop(depth + level, depth + rows - level)
        def _(i, level=level):
            advance(level, i)

    count = count_ref[0]
    lane = lax.broadcasted_iota(jnp.int32, (1, width), 1)

    def react(first, second):
        conc = jnp.concatenate([lev[depth, first], lev[depth, second]], axis=1)
        cell = jnp.concatenate(
            [(first - depth) * width + lane, (second - depth) * width + lane], axis=1
        )
        mask = jnp.where(cell < count, 1.0, 0.0)
        for step in range(CHEM_STEPS):
            high = conc.astype(jnp.bfloat16)
            low = (conc - high.astype(jnp.float32)).astype(jnp.bfloat16)
            terms = jnp.dot(
                weights[...],
                jnp.concatenate([high, high], axis=0),
                preferred_element_type=jnp.float32,
            ) + jnp.dot(
                weights[...],
                jnp.concatenate([low, low], axis=0),
                preferred_element_type=jnp.float32,
            )
            rate = terms[:species]
            for p in range(pairs):
                one = (1 + p) * species
                two = (1 + pairs + p) * species
                rate += terms[one : one + species] * terms[two : two + species]
            conc = conc + rate * mask
        done[first - depth] = conc[:, :width]
        done[second - depth] = conc[:, width:]
        for i in (first, second):
            out_copy(i - depth).start()

    def out_copy(r):
        return pltpu.make_async_copy(done.at[r], tracers_out.at[:, r, :], out_sem.at[r])

    @pl.loop(0, (rows - 2 * depth) // 2)
    def _(i):
        react(2 * depth + 2 * i, 2 * depth + 2 * i + 1)

    @pl.loop(0, depth)
    def _(k):
        for side in range(2):
            halo_send(side, k).wait()
        for level in range(1, depth + 1):
            advance(level, depth - 1 - k + level)
            advance(level, depth + rows + k - level)
        react(2 * depth - 1 - k, rows + k)

    for r in range(rows):
        out_copy(r).wait()
    wind_copy.wait()


def on_device(sizes, tracers, winds, linear, loss, left, right, active):
    species, rows, width = tracers.shape
    pairs = left.shape[0]
    held = rows + 2 * SUBS
    wrows = rows + 2 * (-(-(SUBS + WIND_STAGES) // 8) * 8)
    f32 = jnp.float32
    dma = pltpu.SemaphoreType.DMA
    anywhere = pl.BlockSpec(memory_space=pl.ANY)
    return pl.pallas_call(
        functools.partial(kernel, sizes),
        out_shape=(
            jax.ShapeDtypeStruct(tracers.shape, f32),
            jax.ShapeDtypeStruct(winds.shape, f32),
        ),
        in_specs=[pl.BlockSpec(memory_space=pltpu.SMEM)] + [anywhere] * 6,
        out_specs=(anywhere, anywhere),
        scratch_shapes=[
            pltpu.VMEM((SUBS + 1, held, species, width), f32),
            pltpu.VMEM((2, wrows, width), f32),
            pltpu.VMEM(winds.shape, f32),
            pltpu.VMEM((5, wrows, width), f32),
            pltpu.VMEM(linear.shape, f32),
            pltpu.VMEM((1, species), f32),
            pltpu.VMEM((2,) + left.shape, f32),
            pltpu.VMEM(((1 + 2 * pairs) * species, 2 * species), jnp.bfloat16),
            pltpu.VMEM((rows, species, width), f32),
            dma((rows,)),
            dma((4,)),
            dma,
            dma((rows,)),
            dma,
            dma((2, SUBS)),
            dma((2, SUBS)),
            dma((2,)),
            dma((2,)),
        ],
        compiler_params=pltpu.CompilerParams(collective_id=0, has_side_effects=True),
    )(active, tracers, winds, linear, loss.reshape(1, species), left, right)


def solution(mesh):
    sizes = tuple(mesh.shape[axis] for axis in AXES)
    banded = P(None, AXES, None)
    return jax.shard_map(
        functools.partial(on_device, sizes),
        mesh=mesh,
        in_specs=(banded, banded, P(), P(), P(), P(), P(AXES)),
        out_specs=(banded, banded),
        check_vma=False,
    )
```

```python
import functools

import jax
import jax.numpy as jnp
from jax import lax
from jax.experimental import pallas as pl
from jax.experimental.pallas import tpu as pltpu
from jax.sharding import PartitionSpec as P

SUBS = 4
CHEM_STEPS = 3
WIND_STAGES = 3

DT_WIND = 0.1
VISCOSITY = 0.2
DT_TRACER = 0.1
DT_CHEM = 0.1

AXES = ("tile", "trac")
MESH = pl.DeviceIdType.MESH


def kernel(
    sizes,
    count_ref,
    tracers,
    winds,
    linear,
    loss,
    left,
    right,
    done,
    wind_new,
    lev,
    wind,
    coef,
    lin_v,
    loss_v,
    fac_v,
    weights,
    row_sem,
    par_sem,
    wind_sem,
    send_sem,
    recv_sem,
    wsend_sem,
    wrecv_sem,
):
    tiles, tracs = sizes
    species, rows, width = tracers.shape
    pairs = left.shape[0]
    depth = SUBS
    reach = SUBS + WIND_STAGES
    wrows = wind.shape[1]
    base = (wrows - rows) // 2
    shift = base - depth
    devices = tiles * tracs
    me = lax.axis_index(AXES[0]) * tracs + lax.axis_index(AXES[1])
    up_flat = lax.rem(me + 1, devices)
    down_flat = lax.rem(me + devices - 1, devices)
    up = (up_flat // tracs, lax.rem(up_flat, tracs))
    down = (down_flat // tracs, lax.rem(down_flat, tracs))

    barrier = pltpu.get_barrier_semaphore()
    for neighbour in (up, down):
        pl.semaphore_signal(barrier, inc=1, device_id=neighbour, device_id_type=MESH)

    order = []
    for k in range(depth):
        order += [rows - 1 - k, k]
    order += list(range(depth, rows - depth))

    def row_copy(r):
        return pltpu.make_async_copy(tracers.at[:, r, :], lev.at[0, depth + r], row_sem.at[r])

    own_wind = pltpu.make_async_copy(winds, wind.at[:, base : base + rows, :], wind_sem)
    own_wind.start()
    for r in order:
        row_copy(r).start()
    params = [
        pltpu.make_async_copy(linear, lin_v, par_sem.at[0]),
        pltpu.make_async_copy(loss, loss_v, par_sem.at[1]),
        pltpu.make_async_copy(left, fac_v.at[0], par_sem.at[2]),
        pltpu.make_async_copy(right, fac_v.at[1], par_sem.at[3]),
    ]
    for copy in params:
        copy.start()

    def wind_send(side):
        first = rows - reach if side == 0 else 0
        there = base - reach if side == 0 else base + rows
        return pltpu.make_async_remote_copy(
            src_ref=winds.at[:, first : first + reach, :],
            dst_ref=wind.at[:, there : there + reach, :],
            send_sem=wsend_sem.at[side],
            recv_sem=wrecv_sem.at[side],
            device_id=up if side == 0 else down,
            device_id_type=MESH,
        )

    def halo_send(side, k):
        here = depth + rows - 1 - k if side == 0 else depth + k
        there = depth - 1 - k if side == 0 else depth + rows + k
        return pltpu.make_async_remote_copy(
            src_ref=lev.at[0, here],
            dst_ref=lev.at[0, there],
            send_sem=send_sem.at[side, k],
            recv_sem=recv_sem.at[side, k],
            device_id=up if side == 0 else down,
            device_id_type=MESH,
        )

    def edge_send(side, k):
        row_copy(rows - 1 - k if side == 0 else k).wait()
        halo_send(side, k).start()

    pl.semaphore_wait(barrier, 2)
    for side in range(2):
        wind_send(side).start()
    for k in range(depth):
        for side in range(2):
            edge_send(side, k)

    for copy in params:
        copy.wait()
    diag = lax.broadcasted_iota(jnp.int32, (species, species), 0) == lax.broadcasted_iota(
        jnp.int32, (species, species), 1
    )

    def put(slot, value):
        high = value.astype(jnp.bfloat16)
        low = (value - high.astype(jnp.float32)).astype(jnp.bfloat16)
        lines = pl.ds(slot * species, species)
        weights[lines, :species] = high
        weights[lines, species : 2 * species] = low

    put(0, DT_CHEM * (lin_v[...] - jnp.where(diag, loss_v[...], 0.0)))
    for p in range(pairs):
        put(1 + p, DT_CHEM * fac_v[0, p])
        put(1 + pairs + p, fac_v[1, p])

    for r in range(depth, rows - depth):
        row_copy(r).wait()
    own_wind.wait()

    def update_winds(lines):
        raw = wind[:, lines]
        u0, v0 = raw[0], raw[1]
        held = u0.shape[0]

        def tendency(u, v):
            def of(f):
                east = pltpu.roll(f, width - 1, 1)
                west = pltpu.roll(f, 1, 1)
                north = pltpu.roll(f, held - 1, 0)
                south = pltpu.roll(f, 1, 0)
                along = (east - west) * 0.5
                across = (north - south) * 0.5
                spread = east + west + north + south - 4.0 * f
                return -(u * along + v * across) + VISCOSITY * spread

            return of(u), of(v)

        tu, tv = tendency(u0, v0)
        u1, v1 = u0 + DT_WIND * tu, v0 + DT_WIND * tv
        tu, tv = tendency(u1, v1)
        u2 = 0.75 * u0 + 0.25 * (u1 + DT_WIND * tu)
        v2 = 0.75 * v0 + 0.25 * (v1 + DT_WIND * tv)
        tu, tv = tendency(u2, v2)
        u3 = u0 / 3.0 + 2.0 / 3.0 * (u2 + DT_WIND * tu)
        v3 = v0 / 3.0 + 2.0 / 3.0 * (v2 + DT_WIND * tv)
        if held == wrows:
            wind_new[0] = u3[base : base + rows]
            wind_new[1] = v3[base : base + rows]
        coef[0, lines] = 1.0 - DT_TRACER * (jnp.abs(u3) + jnp.abs(v3))
        coef[1, lines] = pltpu.roll(DT_TRACER * jnp.maximum(u3, 0.0), 1, 1)
        coef[2, lines] = pltpu.roll(-DT_TRACER * jnp.minimum(u3, 0.0), width - 1, 1)
        coef[3, lines] = pltpu.roll(DT_TRACER * jnp.maximum(v3, 0.0), 1, 0)
        coef[4, lines] = pltpu.roll(-DT_TRACER * jnp.minimum(v3, 0.0), held - 1, 0)

    def advance(level, i):
        line = pl.ds(i + shift, 1)
        q = lev[level - 1, i]
        moved = coef[0, line, :] * q
        moved += coef[1, line, :] * pltpu.roll(q, 1, 1)
        moved += coef[2, line, :] * pltpu.roll(q, width - 1, 1)
        moved += coef[3, line, :] * lev[level - 1, i - 1]
        moved += coef[4, line, :] * lev[level - 1, i + 1]
        lev[level, i] = moved

    def sweep(level, first, last):
        @pl.loop(first, last)
        def _(i):
            advance(level, i)

    count = count_ref[0]
    lane = lax.broadcasted_iota(jnp.int32, (1, width), 1)

    def react(first, second):
        conc = jnp.concatenate([lev[depth, first], lev[depth, second]], axis=1)
        cell = jnp.concatenate(
            [(first - depth) * width + lane, (second - depth) * width + lane], axis=1
        )
        mask = jnp.where(cell < count, 1.0, 0.0)
        for step in range(CHEM_STEPS):
            high = conc.astype(jnp.bfloat16)
            low = (conc - high.astype(jnp.float32)).astype(jnp.bfloat16)
            terms = jnp.dot(
                weights[...],
                jnp.concatenate([high, high], axis=0),
                preferred_element_type=jnp.float32,
            ) + jnp.dot(
                weights[...],
                jnp.concatenate([low, low], axis=0),
                preferred_element_type=jnp.float32,
            )
            rate = terms[:species]
            for p in range(pairs):
                one = (1 + p) * species
                two = (1 + pairs + p) * species
                rate += terms[one : one + species] * terms[two : two + species]
            conc = conc + rate * mask
        done[first - depth] = conc[:, :width]
        done[second - depth] = conc[:, width:]

    update_winds(slice(base, base + rows))
    low, high = depth, depth + rows
    for level in range(1, depth + 1):
        sweep(level, low + WIND_STAGES + level, high - WIND_STAGES - level)
    middle = range(low + reach, high - reach, 2)
    for i in middle:
        react(i, i + 1)

    for side in range(2):
        wind_send(side).wait()
    update_winds(slice(0, wrows))
    for level in range(1, depth + 1):
        sweep(level, low + level, low + WIND_STAGES + level)
        sweep(level, high - WIND_STAGES - level, high - level)

    @pl.loop(0, WIND_STAGES)
    def _(i):
        react(low + depth + i, high - depth - 1 - i)

    for k in range(depth):
        for side in range(2):
            halo_send(side, k).wait()
        for level in range(1, depth + 1):
            advance(level, low - 1 - k + level)
            advance(level, high + k - level)
        react(low + depth - 1 - k, high - depth + k)


def finish(done, wind_new, tracers_out, winds_out, out_sem, wind_sem):
    copies = [pltpu.make_async_copy(wind_new, winds_out, wind_sem)]
    for r in range(done.shape[0]):
        copies.append(pltpu.make_async_copy(done.at[r], tracers_out.at[:, r, :], out_sem.at[r]))
    for copy in copies:
        copy.start()
    for copy in copies:
        copy.wait()


def on_device(sizes, tracers, winds, linear, loss, left, right, active):
    species, rows, width = tracers.shape
    pairs = left.shape[0]
    held = rows + 2 * SUBS
    wrows = rows + 2 * (-(-(SUBS + WIND_STAGES) // 8) * 8)
    f32 = jnp.float32
    dma = pltpu.SemaphoreType.DMA
    anywhere = pl.BlockSpec(memory_space=pl.ANY)
    vmem = pl.BlockSpec(memory_space=pltpu.VMEM)
    done, wind_new = pl.pallas_call(
        functools.partial(kernel, sizes),
        out_shape=(
            pltpu.VMEM((rows, species, width), f32),
            pltpu.VMEM(winds.shape, f32),
        ),
        in_specs=[pl.BlockSpec(memory_space=pltpu.SMEM)] + [anywhere] * 6,
        out_specs=(vmem, vmem),
        scratch_shapes=[
            pltpu.VMEM((SUBS + 1, held, species, width), f32),
            pltpu.VMEM((2, wrows, width), f32),
            pltpu.VMEM((5, wrows, width), f32),
            pltpu.VMEM(linear.shape, f32),
            pltpu.VMEM((1, species), f32),
            pltpu.VMEM((2,) + left.shape, f32),
            pltpu.VMEM(((1 + 2 * pairs) * species, 2 * species), jnp.bfloat16),
            dma((rows,)),
            dma((4,)),
            dma,
            dma((2, SUBS)),
            dma((2, SUBS)),
            dma((2,)),
            dma((2,)),
        ],
        compiler_params=pltpu.CompilerParams(collective_id=0, has_side_effects=True),
    )(active, tracers, winds, linear, loss.reshape(1, species), left, right)
    return pl.pallas_call(
        finish,
        out_shape=(
            jax.ShapeDtypeStruct(tracers.shape, f32),
            jax.ShapeDtypeStruct(winds.shape, f32),
        ),
        in_specs=[vmem, vmem],
        out_specs=(anywhere, anywhere),
        scratch_shapes=[dma((rows,)), dma],
    )(
        pltpu.with_memory_space_constraint(done, pltpu.VMEM),
        pltpu.with_memory_space_constraint(wind_new, pltpu.VMEM),
    )


def solution(mesh):
    sizes = tuple(mesh.shape[axis] for axis in AXES)
    banded = P(None, AXES, None)
    return jax.shard_map(
        functools.partial(on_device, sizes),
        mesh=mesh,
        in_specs=(banded, banded, P(), P(), P(), P(), P(AXES)),
        out_specs=(banded, banded),
        check_vma=False,
    )
```

```python
import functools

import jax
import jax.numpy as jnp
from jax import lax
from jax.experimental import pallas as pl
from jax.experimental.pallas import tpu as pltpu
from jax.sharding import PartitionSpec as P

SUBS = 4
CHEM_STEPS = 3
WIND_STAGES = 3

DT_WIND = 0.1
VISCOSITY = 0.2
DT_TRACER = 0.1
DT_CHEM = 0.1

AXES = ("tile", "trac")
MESH = pl.DeviceIdType.MESH


def kernel(
    sizes,
    count_ref,
    tracers,
    winds,
    linear,
    loss,
    left,
    right,
    done,
    wind_new,
    lev,
    wind,
    coef,
    lin_v,
    loss_v,
    fac_v,
    weights,
    row_sem,
    par_sem,
    wind_sem,
    send_sem,
    recv_sem,
    wsend_sem,
    wrecv_sem,
):
    tiles, tracs = sizes
    species, rows, width = tracers.shape
    pairs = left.shape[0]
    depth = SUBS
    reach = SUBS + WIND_STAGES
    wrows = wind.shape[1]
    base = (wrows - rows) // 2
    shift = base - depth
    devices = tiles * tracs
    me = lax.axis_index(AXES[0]) * tracs + lax.axis_index(AXES[1])
    up_flat = lax.rem(me + 1, devices)
    down_flat = lax.rem(me + devices - 1, devices)
    up = (up_flat // tracs, lax.rem(up_flat, tracs))
    down = (down_flat // tracs, lax.rem(down_flat, tracs))

    barrier = pltpu.get_barrier_semaphore()
    for neighbour in (up, down):
        pl.semaphore_signal(barrier, inc=1, device_id=neighbour, device_id_type=MESH)

    order = []
    for k in range(depth):
        order += [rows - 1 - k, k]
    order += list(range(depth, rows - depth))

    def row_copy(r):
        return pltpu.make_async_copy(tracers.at[:, r, :], lev.at[0, depth + r], row_sem.at[r])

    own_wind = pltpu.make_async_copy(winds, wind.at[:, base : base + rows, :], wind_sem)
    own_wind.start()
    for r in order:
        row_copy(r).start()
    params = [
        pltpu.make_async_copy(linear, lin_v, par_sem.at[0]),
        pltpu.make_async_copy(loss, loss_v, par_sem.at[1]),
        pltpu.make_async_copy(left, fac_v.at[0], par_sem.at[2]),
        pltpu.make_async_copy(right, fac_v.at[1], par_sem.at[3]),
    ]
    for copy in params:
        copy.start()

    def wind_send(side):
        first = rows - reach if side == 0 else 0
        there = base - reach if side == 0 else base + rows
        return pltpu.make_async_remote_copy(
            src_ref=winds.at[:, first : first + reach, :],
            dst_ref=wind.at[:, there : there + reach, :],
            send_sem=wsend_sem.at[side],
            recv_sem=wrecv_sem.at[side],
            device_id=up if side == 0 else down,
            device_id_type=MESH,
        )

    def halo_send(side, k):
        here = depth + rows - 1 - k if side == 0 else depth + k
        there = depth - 1 - k if side == 0 else depth + rows + k
        return pltpu.make_async_remote_copy(
            src_ref=lev.at[0, here],
            dst_ref=lev.at[0, there],
            send_sem=send_sem.at[side, k],
            recv_sem=recv_sem.at[side, k],
            device_id=up if side == 0 else down,
            device_id_type=MESH,
        )

    def send_all():
        pl.semaphore_wait(barrier, 2)
        for side in range(2):
            wind_send(side).start()
        for k in range(depth):
            for side in range(2):
                halo_send(side, k).start()

    place = lax.axis_index(AXES[1])
    inside = jnp.logical_and(place > 0, place < tracs - 1)
    for r in order[: 2 * depth]:
        row_copy(r).wait()
    pl.when(inside)(send_all)

    for copy in params:
        copy.wait()
    diag = lax.broadcasted_iota(jnp.int32, (species, species), 0) == lax.broadcasted_iota(
        jnp.int32, (species, species), 1
    )

    def put(slot, value):
        high = value.astype(jnp.bfloat16)
        low = (value - high.astype(jnp.float32)).astype(jnp.bfloat16)
        lines = pl.ds(slot * species, species)
        weights[lines, :species] = high
        weights[lines, species : 2 * species] = low

    put(0, DT_CHEM * (lin_v[...] - jnp.where(diag, loss_v[...], 0.0)))
    for p in range(pairs):
        put(1 + p, DT_CHEM * fac_v[0, p])
        put(1 + pairs + p, fac_v[1, p])

    for r in range(depth, rows - depth):
        row_copy(r).wait()
    own_wind.wait()

    def update_winds(lines):
        raw = wind[:, lines]
        u0, v0 = raw[0], raw[1]
        held = u0.shape[0]

        def tendency(u, v):
            def of(f):
                east = pltpu.roll(f, width - 1, 1)
                west = pltpu.roll(f, 1, 1)
                north = pltpu.roll(f, held - 1, 0)
                south = pltpu.roll(f, 1, 0)
                along = (east - west) * 0.5
                across = (north - south) * 0.5
                spread = east + west + north + south - 4.0 * f
                return -(u * along + v * across) + VISCOSITY * spread

            return of(u), of(v)

        tu, tv = tendency(u0, v0)
        u1, v1 = u0 + DT_WIND * tu, v0 + DT_WIND * tv
        tu, tv = tendency(u1, v1)
        u2 = 0.75 * u0 + 0.25 * (u1 + DT_WIND * tu)
        v2 = 0.75 * v0 + 0.25 * (v1 + DT_WIND * tv)
        tu, tv = tendency(u2, v2)
        u3 = u0 / 3.0 + 2.0 / 3.0 * (u2 + DT_WIND * tu)
        v3 = v0 / 3.0 + 2.0 / 3.0 * (v2 + DT_WIND * tv)
        if held == wrows:
            wind_new[0] = u3[base : base + rows]
            wind_new[1] = v3[base : base + rows]
        coef[0, lines] = 1.0 - DT_TRACER * (jnp.abs(u3) + jnp.abs(v3))
        coef[1, lines] = pltpu.roll(DT_TRACER * jnp.maximum(u3, 0.0), 1, 1)
        coef[2, lines] = pltpu.roll(-DT_TRACER * jnp.minimum(u3, 0.0), width - 1, 1)
        coef[3, lines] = pltpu.roll(DT_TRACER * jnp.maximum(v3, 0.0), 1, 0)
        coef[4, lines] = pltpu.roll(-DT_TRACER * jnp.minimum(v3, 0.0), held - 1, 0)

    def advance(level, i):
        line = pl.ds(i + shift, 1)
        q = lev[level - 1, i]
        moved = coef[0, line, :] * q
        moved += coef[1, line, :] * pltpu.roll(q, 1, 1)
        moved += coef[2, line, :] * pltpu.roll(q, width - 1, 1)
        moved += coef[3, line, :] * lev[level - 1, i - 1]
        moved += coef[4, line, :] * lev[level - 1, i + 1]
        lev[level, i] = moved

    def sweep(level, first, last):
        @pl.loop(first, last)
        def _(i):
            advance(level, i)

    count = count_ref[0]
    lane = lax.broadcasted_iota(jnp.int32, (1, width), 1)

    def react(*couples):
        concs, masks = [], []
        for first, second in couples:
            concs.append(jnp.concatenate([lev[depth, first], lev[depth, second]], axis=1))
            cell = jnp.concatenate(
                [(first - depth) * width + lane, (second - depth) * width + lane], axis=1
            )
            masks.append(jnp.where(cell < count, 1.0, 0.0))
        for step in range(CHEM_STEPS):
            for j, mask in enumerate(masks):
                conc = concs[j]
                high = conc.astype(jnp.bfloat16)
                low = (conc - high.astype(jnp.float32)).astype(jnp.bfloat16)
                terms = jnp.dot(
                    weights[...],
                    jnp.concatenate([high, high], axis=0),
                    preferred_element_type=jnp.float32,
                ) + jnp.dot(
                    weights[...],
                    jnp.concatenate([low, low], axis=0),
                    preferred_element_type=jnp.float32,
                )
                rate = terms[:species]
                for p in range(pairs):
                    one = (1 + p) * species
                    two = (1 + pairs + p) * species
                    rate += terms[one : one + species] * terms[two : two + species]
                concs[j] = conc + rate * mask
        for (first, second), conc in zip(couples, concs):
            done[first - depth] = conc[:, :width]
            done[second - depth] = conc[:, width:]

    update_winds(slice(base, base + rows))
    low, high = depth, depth + rows
    for level in range(1, depth + 1):
        sweep(level, low + WIND_STAGES + level, high - WIND_STAGES - level)
    middle = range(low + reach, high - reach, 2)
    for i in middle:
        react((i, i + 1))

    pl.when(jnp.logical_not(inside))(send_all)

    for side in range(2):
        wind_send(side).wait()
    update_winds(slice(0, wrows))
    for level in range(1, depth + 1):
        sweep(level, low + level, low + WIND_STAGES + level)
        sweep(level, high - WIND_STAGES - level, high - level)

    def edge(k):
        for side in range(2):
            halo_send(side, k).wait()
        for level in range(1, depth + 1):
            advance(level, low - 1 - k + level)
            advance(level, high + k - level)

    couples = [(low + depth + i, high - depth - 1 - i) for i in reversed(range(-depth, WIND_STAGES))]
    ready = WIND_STAGES
    for at in range(0, len(couples), 2):
        batch = couples[at : at + 2]
        while ready < at + len(batch):
            edge(ready - WIND_STAGES)
            ready += 1
        react(*batch)


def finish(done, wind_new, tracers_out, winds_out, out_sem, wind_sem):
    copies = [pltpu.make_async_copy(wind_new, winds_out, wind_sem)]
    for r in range(done.shape[0]):
        copies.append(pltpu.make_async_copy(done.at[r], tracers_out.at[:, r, :], out_sem.at[r]))
    for copy in copies:
        copy.start()
    for copy in copies:
        copy.wait()


def on_device(sizes, tracers, winds, linear, loss, left, right, active):
    species, rows, width = tracers.shape
    pairs = left.shape[0]
    held = rows + 2 * SUBS
    wrows = rows + 2 * (-(-(SUBS + WIND_STAGES) // 8) * 8)
    f32 = jnp.float32
    dma = pltpu.SemaphoreType.DMA
    anywhere = pl.BlockSpec(memory_space=pl.ANY)
    vmem = pl.BlockSpec(memory_space=pltpu.VMEM)
    done, wind_new = pl.pallas_call(
        functools.partial(kernel, sizes),
        out_shape=(
            pltpu.VMEM((rows, species, width), f32),
            pltpu.VMEM(winds.shape, f32),
        ),
        in_specs=[pl.BlockSpec(memory_space=pltpu.SMEM)] + [anywhere] * 6,
        out_specs=(vmem, vmem),
        scratch_shapes=[
            pltpu.VMEM((SUBS + 1, held, species, width), f32),
            pltpu.VMEM((2, wrows, width), f32),
            pltpu.VMEM((5, wrows, width), f32),
            pltpu.VMEM(linear.shape, f32),
            pltpu.VMEM((1, species), f32),
            pltpu.VMEM((2,) + left.shape, f32),
            pltpu.VMEM(((1 + 2 * pairs) * species, 2 * species), jnp.bfloat16),
            dma((rows,)),
            dma((4,)),
            dma,
            dma((2, SUBS)),
            dma((2, SUBS)),
            dma((2,)),
            dma((2,)),
        ],
        compiler_params=pltpu.CompilerParams(collective_id=0, has_side_effects=True),
    )(active, tracers, winds, linear, loss.reshape(1, species), left, right)
    return pl.pallas_call(
        finish,
        out_shape=(
            jax.ShapeDtypeStruct(tracers.shape, f32),
            jax.ShapeDtypeStruct(winds.shape, f32),
        ),
        in_specs=[vmem, vmem],
        out_specs=(anywhere, anywhere),
        scratch_shapes=[dma((rows,)), dma],
    )(
        pltpu.with_memory_space_constraint(done, pltpu.VMEM),
        pltpu.with_memory_space_constraint(wind_new, pltpu.VMEM),
    )


def solution(mesh):
    sizes = tuple(mesh.shape[axis] for axis in AXES)
    banded = P(None, AXES, None)
    return jax.shard_map(
        functools.partial(on_device, sizes),
        mesh=mesh,
        in_specs=(banded, banded, P(), P(), P(), P(), P(AXES)),
        out_specs=(banded, banded),
        check_vma=False,
    )
```

```python
import functools

import jax
import jax.numpy as jnp
from jax import lax
from jax.experimental import pallas as pl
from jax.experimental.pallas import tpu as pltpu
from jax.sharding import PartitionSpec as P

SUBS = 4
CHEM_STEPS = 3
WIND_STAGES = 3
PARTS = 2
BATCH = 1

DT_WIND = 0.1
VISCOSITY = 0.2
DT_TRACER = 0.1
DT_CHEM = 0.1

AXES = ("tile", "trac")
MESH = pl.DeviceIdType.MESH


def kernel(
    sizes,
    count_ref,
    tracers,
    winds,
    linear,
    loss,
    left,
    right,
    done,
    wind_new,
    lev,
    wind,
    coef,
    lin_v,
    loss_v,
    fac_v,
    weights,
    row_sem,
    par_sem,
    wind_sem,
    send_sem,
    recv_sem,
    wsend_sem,
    wrecv_sem,
):
    tiles, tracs = sizes
    species, rows, width = tracers.shape
    pairs = left.shape[0]
    depth = SUBS
    reach = SUBS + WIND_STAGES
    wrows = wind.shape[1]
    base = (wrows - rows) // 2
    shift = base - depth
    devices = tiles * tracs
    me = lax.axis_index(AXES[0]) * tracs + lax.axis_index(AXES[1])
    up_flat = lax.rem(me + 1, devices)
    down_flat = lax.rem(me + devices - 1, devices)
    up = (up_flat // tracs, lax.rem(up_flat, tracs))
    down = (down_flat // tracs, lax.rem(down_flat, tracs))

    barrier = pltpu.get_barrier_semaphore()
    for neighbour in (up, down):
        pl.semaphore_signal(barrier, inc=1, device_id=neighbour, device_id_type=MESH)

    order = []
    for k in range(depth):
        order += [rows - 1 - k, k]
    order += list(range(depth, rows - depth))

    def row_copy(r):
        return pltpu.make_async_copy(tracers.at[:, r, :], lev.at[0, depth + r], row_sem.at[r])

    own_wind = pltpu.make_async_copy(winds, wind.at[:, base : base + rows, :], wind_sem)
    own_wind.start()
    for r in order:
        row_copy(r).start()
    params = [
        pltpu.make_async_copy(linear, lin_v, par_sem.at[0]),
        pltpu.make_async_copy(loss, loss_v, par_sem.at[1]),
        pltpu.make_async_copy(left, fac_v.at[0], par_sem.at[2]),
        pltpu.make_async_copy(right, fac_v.at[1], par_sem.at[3]),
    ]
    for copy in params:
        copy.start()

    def wind_send(side):
        first = rows - reach if side == 0 else 0
        there = base - reach if side == 0 else base + rows
        return pltpu.make_async_remote_copy(
            src_ref=winds.at[:, first : first + reach, :],
            dst_ref=wind.at[:, there : there + reach, :],
            send_sem=wsend_sem.at[side],
            recv_sem=wrecv_sem.at[side],
            device_id=up if side == 0 else down,
            device_id_type=MESH,
        )

    def halo_send(side, k):
        here = depth + rows - 1 - k if side == 0 else depth + k
        there = depth - 1 - k if side == 0 else depth + rows + k
        return pltpu.make_async_remote_copy(
            src_ref=lev.at[0, here],
            dst_ref=lev.at[0, there],
            send_sem=send_sem.at[side, k],
            recv_sem=recv_sem.at[side, k],
            device_id=up if side == 0 else down,
            device_id_type=MESH,
        )

    def send_all():
        pl.semaphore_wait(barrier, 2)
        for side in range(2):
            wind_send(side).start()
        for k in range(depth):
            for side in range(2):
                halo_send(side, k).start()

    place = lax.axis_index(AXES[1])
    inside = jnp.logical_and(place > 0, place < tracs - 1)
    for r in order[: 2 * depth]:
        row_copy(r).wait()
    pl.when(inside)(send_all)

    for copy in params:
        copy.wait()
    diag = lax.broadcasted_iota(jnp.int32, (species, species), 0) == lax.broadcasted_iota(
        jnp.int32, (species, species), 1
    )

    block = species // PARTS
    height = (1 + 2 * pairs) * block

    def put(slot, value):
        high = value.astype(jnp.bfloat16)
        low = (value - high.astype(jnp.float32)).astype(jnp.bfloat16)
        for part in range(PARTS):
            lines = pl.ds((part * (1 + 2 * pairs) + slot) * block, block)
            own = slice(part * block, (part + 1) * block)
            weights[lines, :species] = high[own]
            weights[lines, species : 2 * species] = low[own]

    put(0, DT_CHEM * (lin_v[...] - jnp.where(diag, loss_v[...], 0.0)))
    for p in range(pairs):
        put(1 + p, DT_CHEM * fac_v[0, p])
        put(1 + pairs + p, fac_v[1, p])

    for r in range(depth, rows - depth):
        row_copy(r).wait()
    own_wind.wait()

    def update_winds(lines):
        raw = wind[:, lines]
        u0, v0 = raw[0], raw[1]
        held = u0.shape[0]

        def tendency(u, v):
            def of(f):
                east = pltpu.roll(f, width - 1, 1)
                west = pltpu.roll(f, 1, 1)
                north = pltpu.roll(f, held - 1, 0)
                south = pltpu.roll(f, 1, 0)
                along = (east - west) * 0.5
                across = (north - south) * 0.5
                spread = east + west + north + south - 4.0 * f
                return -(u * along + v * across) + VISCOSITY * spread

            return of(u), of(v)

        tu, tv = tendency(u0, v0)
        u1, v1 = u0 + DT_WIND * tu, v0 + DT_WIND * tv
        tu, tv = tendency(u1, v1)
        u2 = 0.75 * u0 + 0.25 * (u1 + DT_WIND * tu)
        v2 = 0.75 * v0 + 0.25 * (v1 + DT_WIND * tv)
        tu, tv = tendency(u2, v2)
        u3 = u0 / 3.0 + 2.0 / 3.0 * (u2 + DT_WIND * tu)
        v3 = v0 / 3.0 + 2.0 / 3.0 * (v2 + DT_WIND * tv)
        if held == wrows:
            wind_new[0] = u3[base : base + rows]
            wind_new[1] = v3[base : base + rows]
        coef[0, lines] = 1.0 - DT_TRACER * (jnp.abs(u3) + jnp.abs(v3))
        coef[1, lines] = pltpu.roll(DT_TRACER * jnp.maximum(u3, 0.0), 1, 1)
        coef[2, lines] = pltpu.roll(-DT_TRACER * jnp.minimum(u3, 0.0), width - 1, 1)
        coef[3, lines] = pltpu.roll(DT_TRACER * jnp.maximum(v3, 0.0), 1, 0)
        coef[4, lines] = pltpu.roll(-DT_TRACER * jnp.minimum(v3, 0.0), held - 1, 0)

    def advance(level, i):
        line = pl.ds(i + shift, 1)
        q = lev[level - 1, i]
        moved = coef[0, line, :] * q
        moved += coef[1, line, :] * pltpu.roll(q, 1, 1)
        moved += coef[2, line, :] * pltpu.roll(q, width - 1, 1)
        moved += coef[3, line, :] * lev[level - 1, i - 1]
        moved += coef[4, line, :] * lev[level - 1, i + 1]
        lev[level, i] = moved

    def sweep(level, first, last):
        @pl.loop(first, last)
        def _(i):
            advance(level, i)

    count = count_ref[0]
    lane = lax.broadcasted_iota(jnp.int32, (1, width), 1)

    def react(*couples):
        concs, masks = [], []
        for first, second in couples:
            concs.append(jnp.concatenate([lev[depth, first], lev[depth, second]], axis=1))
            cell = jnp.concatenate(
                [(first - depth) * width + lane, (second - depth) * width + lane], axis=1
            )
            masks.append(jnp.where(cell < count, 1.0, 0.0))
        for step in range(CHEM_STEPS):
            for j, mask in enumerate(masks):
                conc = concs[j]
                high = conc.astype(jnp.bfloat16)
                low = (conc - high.astype(jnp.float32)).astype(jnp.bfloat16)
                high = jnp.concatenate([high, high], axis=0)
                low = jnp.concatenate([low, low], axis=0)
                blocks = []
                for part in range(PARTS):
                    lhs = weights[part * height : (part + 1) * height]
                    terms = jnp.dot(lhs, high, preferred_element_type=jnp.float32) + jnp.dot(
                        lhs, low, preferred_element_type=jnp.float32
                    )
                    rate = terms[:block]
                    for p in range(pairs):
                        one = (1 + p) * block
                        two = (1 + pairs + p) * block
                        rate += terms[one : one + block] * terms[two : two + block]
                    blocks.append(conc[part * block : (part + 1) * block] + rate * mask)
                concs[j] = jnp.concatenate(blocks, axis=0)
        for (first, second), conc in zip(couples, concs):
            done[first - depth] = conc[:, :width]
            done[second - depth] = conc[:, width:]

    update_winds(slice(base, base + rows))
    low, high = depth, depth + rows
    for level in range(1, depth + 1):
        sweep(level, low + WIND_STAGES + level, high - WIND_STAGES - level)
    middle = range(low + reach, high - reach, 2)
    for i in middle:
        react((i, i + 1))

    pl.when(jnp.logical_not(inside))(send_all)

    for side in range(2):
        wind_send(side).wait()
    update_winds(slice(0, wrows))
    for level in range(1, depth + 1):
        sweep(level, low + level, low + WIND_STAGES + level)
        sweep(level, high - WIND_STAGES - level, high - level)

    def edge(k):
        for side in range(2):
            halo_send(side, k).wait()
        for level in range(1, depth + 1):
            advance(level, low - 1 - k + level)
            advance(level, high + k - level)

    couples = [(low + depth + i, high - depth - 1 - i) for i in reversed(range(-depth, WIND_STAGES))]
    ready = WIND_STAGES
    for at in range(0, len(couples), BATCH):
        batch = couples[at : at + BATCH]
        while ready < at + len(batch):
            edge(ready - WIND_STAGES)
            ready += 1
        react(*batch)


def finish(done, wind_new, tracers_out, winds_out, out_sem, wind_sem):
    copies = [pltpu.make_async_copy(wind_new, winds_out, wind_sem)]
    for r in range(done.shape[0]):
        copies.append(pltpu.make_async_copy(done.at[r], tracers_out.at[:, r, :], out_sem.at[r]))
    for copy in copies:
        copy.start()
    for copy in copies:
        copy.wait()


def on_device(sizes, tracers, winds, linear, loss, left, right, active):
    species, rows, width = tracers.shape
    pairs = left.shape[0]
    held = rows + 2 * SUBS
    wrows = rows + 2 * (-(-(SUBS + WIND_STAGES) // 8) * 8)
    f32 = jnp.float32
    dma = pltpu.SemaphoreType.DMA
    anywhere = pl.BlockSpec(memory_space=pl.ANY)
    vmem = pl.BlockSpec(memory_space=pltpu.VMEM)
    done, wind_new = pl.pallas_call(
        functools.partial(kernel, sizes),
        out_shape=(
            pltpu.VMEM((rows, species, width), f32),
            pltpu.VMEM(winds.shape, f32),
        ),
        in_specs=[pl.BlockSpec(memory_space=pltpu.SMEM)] + [anywhere] * 6,
        out_specs=(vmem, vmem),
        scratch_shapes=[
            pltpu.VMEM((SUBS + 1, held, species, width), f32),
            pltpu.VMEM((2, wrows, width), f32),
            pltpu.VMEM((5, wrows, width), f32),
            pltpu.VMEM(linear.shape, f32),
            pltpu.VMEM((1, species), f32),
            pltpu.VMEM((2,) + left.shape, f32),
            pltpu.VMEM(((1 + 2 * pairs) * species, 2 * species), jnp.bfloat16),
            dma((rows,)),
            dma((4,)),
            dma,
            dma((2, SUBS)),
            dma((2, SUBS)),
            dma((2,)),
            dma((2,)),
        ],
        compiler_params=pltpu.CompilerParams(collective_id=0, has_side_effects=True),
    )(active, tracers, winds, linear, loss.reshape(1, species), left, right)
    return pl.pallas_call(
        finish,
        out_shape=(
            jax.ShapeDtypeStruct(tracers.shape, f32),
            jax.ShapeDtypeStruct(winds.shape, f32),
        ),
        in_specs=[vmem, vmem],
        out_specs=(anywhere, anywhere),
        scratch_shapes=[dma((rows,)), dma],
    )(
        pltpu.with_memory_space_constraint(done, pltpu.VMEM),
        pltpu.with_memory_space_constraint(wind_new, pltpu.VMEM),
    )


def solution(mesh):
    sizes = tuple(mesh.shape[axis] for axis in AXES)
    banded = P(None, AXES, None)
    return jax.shard_map(
        functools.partial(on_device, sizes),
        mesh=mesh,
        in_specs=(banded, banded, P(), P(), P(), P(), P(AXES)),
        out_specs=(banded, banded),
        check_vma=False,
    )
```

```python
import functools

import jax
import jax.numpy as jnp
from jax import lax
from jax.experimental import pallas as pl
from jax.experimental.pallas import tpu as pltpu
from jax.sharding import PartitionSpec as P

SUBS = 4
CHEM_STEPS = 3
WIND_STAGES = 3
PARTS = 2
LEAD = 2
BATCH = 1

DT_WIND = 0.1
VISCOSITY = 0.2
DT_TRACER = 0.1
DT_CHEM = 0.1

AXES = ("tile", "trac")
MESH = pl.DeviceIdType.MESH


def kernel(
    sizes,
    count_ref,
    tracers,
    winds,
    linear,
    loss,
    left,
    right,
    done,
    wind_new,
    lev,
    wind,
    coef,
    lin_v,
    loss_v,
    fac_v,
    weights,
    row_sem,
    par_sem,
    wind_sem,
    send_sem,
    recv_sem,
    wsend_sem,
    wrecv_sem,
):
    tiles, tracs = sizes
    species, rows, width = tracers.shape
    pairs = left.shape[0]
    depth = SUBS
    reach = SUBS + WIND_STAGES
    wrows = wind.shape[1]
    base = (wrows - rows) // 2
    shift = base - depth
    devices = tiles * tracs
    me = lax.axis_index(AXES[0]) * tracs + lax.axis_index(AXES[1])
    up_flat = lax.rem(me + 1, devices)
    down_flat = lax.rem(me + devices - 1, devices)
    up = (up_flat // tracs, lax.rem(up_flat, tracs))
    down = (down_flat // tracs, lax.rem(down_flat, tracs))

    barrier = pltpu.get_barrier_semaphore()
    for neighbour in (up, down):
        pl.semaphore_signal(barrier, inc=1, device_id=neighbour, device_id_type=MESH)

    order = []
    for k in range(depth):
        order += [rows - 1 - k, k]
    order += list(range(depth, rows - depth))

    def row_copy(r):
        return pltpu.make_async_copy(tracers.at[:, r, :], lev.at[0, depth + r], row_sem.at[r])

    own_wind = pltpu.make_async_copy(winds, wind.at[:, base : base + rows, :], wind_sem)
    own_wind.start()
    for r in order:
        row_copy(r).start()
    params = [
        pltpu.make_async_copy(linear, lin_v, par_sem.at[0]),
        pltpu.make_async_copy(loss, loss_v, par_sem.at[1]),
        pltpu.make_async_copy(left, fac_v.at[0], par_sem.at[2]),
        pltpu.make_async_copy(right, fac_v.at[1], par_sem.at[3]),
    ]
    for copy in params:
        copy.start()

    def wind_send(side):
        first = rows - reach if side == 0 else 0
        there = base - reach if side == 0 else base + rows
        return pltpu.make_async_remote_copy(
            src_ref=winds.at[:, first : first + reach, :],
            dst_ref=wind.at[:, there : there + reach, :],
            send_sem=wsend_sem.at[side],
            recv_sem=wrecv_sem.at[side],
            device_id=up if side == 0 else down,
            device_id_type=MESH,
        )

    def halo_send(side, k):
        here = depth + rows - 1 - k if side == 0 else depth + k
        there = depth - 1 - k if side == 0 else depth + rows + k
        return pltpu.make_async_remote_copy(
            src_ref=lev.at[0, here],
            dst_ref=lev.at[0, there],
            send_sem=send_sem.at[side, k],
            recv_sem=recv_sem.at[side, k],
            device_id=up if side == 0 else down,
            device_id_type=MESH,
        )

    for r in order[: 2 * depth]:
        row_copy(r).wait()
    pl.semaphore_wait(barrier, 2)
    place = lax.axis_index(AXES[1])
    last = tracs - 1

    @pl.when(jnp.logical_and(place > 0, place < last))
    def _():
        for side in range(2):
            wind_send(side).start()
        for k in range(depth):
            for side in range(2):
                halo_send(side, k).start()

    for end, near in ((0, 0), (last, 1)):

        @pl.when(place == end)
        def _(near=near):
            wind_send(1 - near).start()
            wind_send(near).start()
            for k in range(depth + LEAD):
                if k < depth:
                    halo_send(1 - near, k).start()
                if k >= LEAD:
                    halo_send(near, k - LEAD).start()

    for copy in params:
        copy.wait()
    diag = lax.broadcasted_iota(jnp.int32, (species, species), 0) == lax.broadcasted_iota(
        jnp.int32, (species, species), 1
    )

    block = species // PARTS
    height = (1 + 2 * pairs) * block

    def put(slot, value):
        high = value.astype(jnp.bfloat16)
        low = (value - high.astype(jnp.float32)).astype(jnp.bfloat16)
        for part in range(PARTS):
            lines = pl.ds((part * (1 + 2 * pairs) + slot) * block, block)
            own = slice(part * block, (part + 1) * block)
            weights[lines, :species] = high[own]
            weights[lines, species : 2 * species] = low[own]

    put(0, DT_CHEM * (lin_v[...] - jnp.where(diag, loss_v[...], 0.0)))
    for p in range(pairs):
        put(1 + p, DT_CHEM * fac_v[0, p])
        put(1 + pairs + p, fac_v[1, p])

    for r in range(depth, rows - depth):
        row_copy(r).wait()
    own_wind.wait()

    def update_winds(lines):
        raw = wind[:, lines]
        u0, v0 = raw[0], raw[1]
        held = u0.shape[0]

        def tendency(u, v):
            def of(f):
                east = pltpu.roll(f, width - 1, 1)
                west = pltpu.roll(f, 1, 1)
                north = pltpu.roll(f, held - 1, 0)
                south = pltpu.roll(f, 1, 0)
                along = (east - west) * 0.5
                across = (north - south) * 0.5
                spread = east + west + north + south - 4.0 * f
                return -(u * along + v * across) + VISCOSITY * spread

            return of(u), of(v)

        tu, tv = tendency(u0, v0)
        u1, v1 = u0 + DT_WIND * tu, v0 + DT_WIND * tv
        tu, tv = tendency(u1, v1)
        u2 = 0.75 * u0 + 0.25 * (u1 + DT_WIND * tu)
        v2 = 0.75 * v0 + 0.25 * (v1 + DT_WIND * tv)
        tu, tv = tendency(u2, v2)
        u3 = u0 / 3.0 + 2.0 / 3.0 * (u2 + DT_WIND * tu)
        v3 = v0 / 3.0 + 2.0 / 3.0 * (v2 + DT_WIND * tv)
        if held == wrows:
            wind_new[0] = u3[base : base + rows]
            wind_new[1] = v3[base : base + rows]
        coef[0, lines] = 1.0 - DT_TRACER * (jnp.abs(u3) + jnp.abs(v3))
        coef[1, lines] = pltpu.roll(DT_TRACER * jnp.maximum(u3, 0.0), 1, 1)
        coef[2, lines] = pltpu.roll(-DT_TRACER * jnp.minimum(u3, 0.0), width - 1, 1)
        coef[3, lines] = pltpu.roll(DT_TRACER * jnp.maximum(v3, 0.0), 1, 0)
        coef[4, lines] = pltpu.roll(-DT_TRACER * jnp.minimum(v3, 0.0), held - 1, 0)

    def advance(level, i):
        line = pl.ds(i + shift, 1)
        q = lev[level - 1, i]
        moved = coef[0, line, :] * q
        moved += coef[1, line, :] * pltpu.roll(q, 1, 1)
        moved += coef[2, line, :] * pltpu.roll(q, width - 1, 1)
        moved += coef[3, line, :] * lev[level - 1, i - 1]
        moved += coef[4, line, :] * lev[level - 1, i + 1]
        lev[level, i] = moved

    def sweep(level, first, last):
        @pl.loop(first, last)
        def _(i):
            advance(level, i)

    count = count_ref[0]
    lane = lax.broadcasted_iota(jnp.int32, (1, width), 1)

    def react(*couples):
        concs, masks = [], []
        for first, second in couples:
            concs.append(jnp.concatenate([lev[depth, first], lev[depth, second]], axis=1))
            cell = jnp.concatenate(
                [(first - depth) * width + lane, (second - depth) * width + lane], axis=1
            )
            masks.append(jnp.where(cell < count, 1.0, 0.0))
        for step in range(CHEM_STEPS):
            for j, mask in enumerate(masks):
                conc = concs[j]
                high = conc.astype(jnp.bfloat16)
                low = (conc - high.astype(jnp.float32)).astype(jnp.bfloat16)
                high = jnp.concatenate([high, high], axis=0)
                low = jnp.concatenate([low, low], axis=0)
                blocks = []
                for part in range(PARTS):
                    lhs = weights[part * height : (part + 1) * height]
                    terms = jnp.dot(lhs, high, preferred_element_type=jnp.float32) + jnp.dot(
                        lhs, low, preferred_element_type=jnp.float32
                    )
                    rate = terms[:block]
                    for p in range(pairs):
                        one = (1 + p) * block
                        two = (1 + pairs + p) * block
                        rate += terms[one : one + block] * terms[two : two + block]
                    blocks.append(conc[part * block : (part + 1) * block] + rate * mask)
                concs[j] = jnp.concatenate(blocks, axis=0)
        for (first, second), conc in zip(couples, concs):
            done[first - depth] = conc[:, :width]
            done[second - depth] = conc[:, width:]

    update_winds(slice(base, base + rows))
    low, high = depth, depth + rows
    for level in range(1, depth + 1):
        sweep(level, low + WIND_STAGES + level, high - WIND_STAGES - level)
    middle = range(low + reach, high - reach, 2)
    for i in middle:
        react((i, i + 1))

    for side in range(2):
        wind_send(side).wait()
    update_winds(slice(0, wrows))
    for level in range(1, depth + 1):
        sweep(level, low + level, low + WIND_STAGES + level)
        sweep(level, high - WIND_STAGES - level, high - level)

    def edge(k):
        for side in range(2):
            halo_send(side, k).wait()
        for level in range(1, depth + 1):
            advance(level, low - 1 - k + level)
            advance(level, high + k - level)

    couples = [(low + depth + i, high - depth - 1 - i) for i in reversed(range(-depth, WIND_STAGES))]
    ready = WIND_STAGES
    for at in range(0, len(couples), BATCH):
        batch = couples[at : at + BATCH]
        while ready < at + len(batch):
            edge(ready - WIND_STAGES)
            ready += 1
        react(*batch)


def finish(done, wind_new, tracers_out, winds_out, out_sem, wind_sem):
    copies = [pltpu.make_async_copy(wind_new, winds_out, wind_sem)]
    for r in range(done.shape[0]):
        copies.append(pltpu.make_async_copy(done.at[r], tracers_out.at[:, r, :], out_sem.at[r]))
    for copy in copies:
        copy.start()
    for copy in copies:
        copy.wait()


def on_device(sizes, tracers, winds, linear, loss, left, right, active):
    species, rows, width = tracers.shape
    pairs = left.shape[0]
    held = rows + 2 * SUBS
    wrows = rows + 2 * (-(-(SUBS + WIND_STAGES) // 8) * 8)
    f32 = jnp.float32
    dma = pltpu.SemaphoreType.DMA
    anywhere = pl.BlockSpec(memory_space=pl.ANY)
    vmem = pl.BlockSpec(memory_space=pltpu.VMEM)
    done, wind_new = pl.pallas_call(
        functools.partial(kernel, sizes),
        out_shape=(
            pltpu.VMEM((rows, species, width), f32),
            pltpu.VMEM(winds.shape, f32),
        ),
        in_specs=[pl.BlockSpec(memory_space=pltpu.SMEM)] + [anywhere] * 6,
        out_specs=(vmem, vmem),
        scratch_shapes=[
            pltpu.VMEM((SUBS + 1, held, species, width), f32),
            pltpu.VMEM((2, wrows, width), f32),
            pltpu.VMEM((5, wrows, width), f32),
            pltpu.VMEM(linear.shape, f32),
            pltpu.VMEM((1, species), f32),
            pltpu.VMEM((2,) + left.shape, f32),
            pltpu.VMEM(((1 + 2 * pairs) * species, 2 * species), jnp.bfloat16),
            dma((rows,)),
            dma((4,)),
            dma,
            dma((2, SUBS)),
            dma((2, SUBS)),
            dma((2,)),
            dma((2,)),
        ],
        compiler_params=pltpu.CompilerParams(collective_id=0, has_side_effects=True),
    )(active, tracers, winds, linear, loss.reshape(1, species), left, right)
    return pl.pallas_call(
        finish,
        out_shape=(
            jax.ShapeDtypeStruct(tracers.shape, f32),
            jax.ShapeDtypeStruct(winds.shape, f32),
        ),
        in_specs=[vmem, vmem],
        out_specs=(anywhere, anywhere),
        scratch_shapes=[dma((rows,)), dma],
    )(
        pltpu.with_memory_space_constraint(done, pltpu.VMEM),
        pltpu.with_memory_space_constraint(wind_new, pltpu.VMEM),
    )


def solution(mesh):
    sizes = tuple(mesh.shape[axis] for axis in AXES)
    banded = P(None, AXES, None)
    return jax.shard_map(
        functools.partial(on_device, sizes),
        mesh=mesh,
        in_specs=(banded, banded, P(), P(), P(), P(), P(AXES)),
        out_specs=(banded, banded),
        check_vma=False,
    )
```

```python
import functools

import jax
import jax.numpy as jnp
from jax import lax
from jax.experimental import pallas as pl
from jax.experimental.pallas import tpu as pltpu
from jax.sharding import PartitionSpec as P

SUBS = 4
CHEM_STEPS = 3
WIND_STAGES = 3
PARTS = 2
LEAD = 2
BATCH = 1

DT_WIND = 0.1
VISCOSITY = 0.2
DT_TRACER = 0.1
DT_CHEM = 0.1

AXES = ("tile", "trac")
MESH = pl.DeviceIdType.MESH


def kernel(
    sizes,
    count_ref,
    tracers,
    winds,
    linear,
    loss,
    left,
    right,
    done,
    wind_new,
    lev,
    wind,
    coef,
    lin_v,
    loss_v,
    fac_v,
    weights,
    row_sem,
    par_sem,
    count_v,
    count_sem,
    wind_sem,
    send_sem,
    recv_sem,
    wsend_sem,
    wrecv_sem,
):
    tiles, tracs = sizes
    species, rows, width = tracers.shape
    pairs = left.shape[0]
    depth = SUBS
    reach = SUBS + WIND_STAGES
    wrows = wind.shape[1]
    base = (wrows - rows) // 2
    shift = base - depth
    devices = tiles * tracs
    me = lax.axis_index(AXES[0]) * tracs + lax.axis_index(AXES[1])
    up_flat = lax.rem(me + 1, devices)
    down_flat = lax.rem(me + devices - 1, devices)
    up = (up_flat // tracs, lax.rem(up_flat, tracs))
    down = (down_flat // tracs, lax.rem(down_flat, tracs))

    barrier = pltpu.get_barrier_semaphore()
    for neighbour in (up, down):
        pl.semaphore_signal(barrier, inc=1, device_id=neighbour, device_id_type=MESH)

    order = []
    for k in range(depth):
        order += [rows - 1 - k, k]
    order += list(range(depth, rows - depth))

    def row_copy(r):
        return pltpu.make_async_copy(tracers.at[:, r, :], lev.at[0, depth + r], row_sem.at[r])

    own_wind = pltpu.make_async_copy(winds, wind.at[:, base : base + rows, :], wind_sem)
    own_wind.start()
    count_copy = pltpu.make_async_copy(count_ref, count_v, count_sem)
    count_copy.start()
    for r in order:
        row_copy(r).start()
    params = [
        pltpu.make_async_copy(linear, lin_v, par_sem.at[0]),
        pltpu.make_async_copy(loss, loss_v, par_sem.at[1]),
        pltpu.make_async_copy(left, fac_v.at[0], par_sem.at[2]),
        pltpu.make_async_copy(right, fac_v.at[1], par_sem.at[3]),
    ]
    for copy in params:
        copy.start()

    def wind_send(side):
        first = rows - reach if side == 0 else 0
        there = base - reach if side == 0 else base + rows
        return pltpu.make_async_remote_copy(
            src_ref=winds.at[:, first : first + reach, :],
            dst_ref=wind.at[:, there : there + reach, :],
            send_sem=wsend_sem.at[side],
            recv_sem=wrecv_sem.at[side],
            device_id=up if side == 0 else down,
            device_id_type=MESH,
        )

    def halo_send(side, k):
        here = depth + rows - 1 - k if side == 0 else depth + k
        there = depth - 1 - k if side == 0 else depth + rows + k
        return pltpu.make_async_remote_copy(
            src_ref=lev.at[0, here],
            dst_ref=lev.at[0, there],
            send_sem=send_sem.at[side, k],
            recv_sem=recv_sem.at[side, k],
            device_id=up if side == 0 else down,
            device_id_type=MESH,
        )

    for r in order[: 2 * depth]:
        row_copy(r).wait()
    pl.semaphore_wait(barrier, 2)
    place = lax.axis_index(AXES[1])
    last = tracs - 1

    @pl.when(jnp.logical_and(place > 0, place < last))
    def _():
        for side in range(2):
            wind_send(side).start()
        for k in range(depth):
            for side in range(2):
                halo_send(side, k).start()

    for end, near in ((0, 0), (last, 1)):

        @pl.when(place == end)
        def _(near=near):
            wind_send(1 - near).start()
            wind_send(near).start()
            for k in range(depth + LEAD):
                if k < depth:
                    halo_send(1 - near, k).start()
                if k >= LEAD:
                    halo_send(near, k - LEAD).start()

    for copy in params:
        copy.wait()
    diag = lax.broadcasted_iota(jnp.int32, (species, species), 0) == lax.broadcasted_iota(
        jnp.int32, (species, species), 1
    )

    block = species // PARTS
    height = (1 + 2 * pairs) * block

    def put(slot, value):
        high = value.astype(jnp.bfloat16)
        low = (value - high.astype(jnp.float32)).astype(jnp.bfloat16)
        for part in range(PARTS):
            lines = pl.ds((part * (1 + 2 * pairs) + slot) * block, block)
            own = slice(part * block, (part + 1) * block)
            weights[lines, :species] = high[own]
            weights[lines, species : 2 * species] = low[own]

    put(0, DT_CHEM * (lin_v[...] - jnp.where(diag, loss_v[...], 0.0)))
    for p in range(pairs):
        put(1 + p, DT_CHEM * fac_v[0, p])
        put(1 + pairs + p, fac_v[1, p])

    for r in range(depth, rows - depth):
        row_copy(r).wait()
    own_wind.wait()

    def update_winds(lines):
        raw = wind[:, lines]
        u0, v0 = raw[0], raw[1]
        held = u0.shape[0]

        def tendency(u, v):
            def of(f):
                east = pltpu.roll(f, width - 1, 1)
                west = pltpu.roll(f, 1, 1)
                north = pltpu.roll(f, held - 1, 0)
                south = pltpu.roll(f, 1, 0)
                along = (east - west) * 0.5
                across = (north - south) * 0.5
                spread = east + west + north + south - 4.0 * f
                return -(u * along + v * across) + VISCOSITY * spread

            return of(u), of(v)

        tu, tv = tendency(u0, v0)
        u1, v1 = u0 + DT_WIND * tu, v0 + DT_WIND * tv
        tu, tv = tendency(u1, v1)
        u2 = 0.75 * u0 + 0.25 * (u1 + DT_WIND * tu)
        v2 = 0.75 * v0 + 0.25 * (v1 + DT_WIND * tv)
        tu, tv = tendency(u2, v2)
        u3 = u0 / 3.0 + 2.0 / 3.0 * (u2 + DT_WIND * tu)
        v3 = v0 / 3.0 + 2.0 / 3.0 * (v2 + DT_WIND * tv)
        if held == wrows:
            wind_new[0] = u3[base : base + rows]
            wind_new[1] = v3[base : base + rows]
        coef[0, lines] = 1.0 - DT_TRACER * (jnp.abs(u3) + jnp.abs(v3))
        coef[1, lines] = pltpu.roll(DT_TRACER * jnp.maximum(u3, 0.0), 1, 1)
        coef[2, lines] = pltpu.roll(-DT_TRACER * jnp.minimum(u3, 0.0), width - 1, 1)
        coef[3, lines] = pltpu.roll(DT_TRACER * jnp.maximum(v3, 0.0), 1, 0)
        coef[4, lines] = pltpu.roll(-DT_TRACER * jnp.minimum(v3, 0.0), held - 1, 0)

    def advance(level, i):
        line = pl.ds(i + shift, 1)
        q = lev[level - 1, i]
        moved = coef[0, line, :] * q
        moved += coef[1, line, :] * pltpu.roll(q, 1, 1)
        moved += coef[2, line, :] * pltpu.roll(q, width - 1, 1)
        moved += coef[3, line, :] * lev[level - 1, i - 1]
        moved += coef[4, line, :] * lev[level - 1, i + 1]
        lev[level, i] = moved

    def sweep(level, first, last):
        @pl.loop(first, last)
        def _(i):
            advance(level, i)

    count_copy.wait()
    count = count_v[0]
    lane = lax.broadcasted_iota(jnp.int32, (1, width), 1)

    def react(*couples):
        concs, masks = [], []
        for first, second in couples:
            concs.append(jnp.concatenate([lev[depth, first], lev[depth, second]], axis=1))
            cell = jnp.concatenate(
                [(first - depth) * width + lane, (second - depth) * width + lane], axis=1
            )
            masks.append(jnp.where(cell < count, 1.0, 0.0))
        for step in range(CHEM_STEPS):
            for j, mask in enumerate(masks):
                conc = concs[j]
                high = conc.astype(jnp.bfloat16)
                low = (conc - high.astype(jnp.float32)).astype(jnp.bfloat16)
                high = jnp.concatenate([high, high], axis=0)
                low = jnp.concatenate([low, low], axis=0)
                blocks = []
                for part in range(PARTS):
                    lhs = weights[part * height : (part + 1) * height]
                    terms = jnp.dot(lhs, high, preferred_element_type=jnp.float32) + jnp.dot(
                        lhs, low, preferred_element_type=jnp.float32
                    )
                    rate = terms[:block]
                    for p in range(pairs):
                        one = (1 + p) * block
                        two = (1 + pairs + p) * block
                        rate += terms[one : one + block] * terms[two : two + block]
                    blocks.append(conc[part * block : (part + 1) * block] + rate * mask)
                concs[j] = jnp.concatenate(blocks, axis=0)
        for (first, second), conc in zip(couples, concs):
            done[first - depth] = conc[:, :width]
            done[second - depth] = conc[:, width:]

    update_winds(slice(base, base + rows))
    low, high = depth, depth + rows
    for level in range(1, depth + 1):
        sweep(level, low + WIND_STAGES + level, high - WIND_STAGES - level)
    middle = range(low + reach, high - reach, 2)
    for i in middle:
        react((i, i + 1))

    for side in range(2):
        wind_send(side).wait()
    update_winds(slice(0, wrows))
    for level in range(1, depth + 1):
        sweep(level, low + level, low + WIND_STAGES + level)
        sweep(level, high - WIND_STAGES - level, high - level)

    def edge(k):
        halo_send(0, k).wait()
        for level in range(1, depth + 1):
            advance(level, low - 1 - k + level)
        halo_send(1, k).wait()
        for level in range(1, depth + 1):
            advance(level, high + k - level)

    couples = [(low + depth + i, high - depth - 1 - i) for i in reversed(range(-depth, WIND_STAGES))]
    ready = WIND_STAGES
    for at in range(0, len(couples), BATCH):
        batch = couples[at : at + BATCH]
        while ready < at + len(batch):
            edge(ready - WIND_STAGES)
            ready += 1
        react(*batch)


def finish(done, wind_new, tracers_out, winds_out, out_sem, wind_sem):
    copies = [pltpu.make_async_copy(wind_new, winds_out, wind_sem)]
    for r in range(done.shape[0]):
        copies.append(pltpu.make_async_copy(done.at[r], tracers_out.at[:, r, :], out_sem.at[r]))
    for copy in copies:
        copy.start()
    for copy in copies:
        copy.wait()


def on_device(sizes, tracers, winds, linear, loss, left, right, active):
    species, rows, width = tracers.shape
    pairs = left.shape[0]
    held = rows + 2 * SUBS
    wrows = rows + 2 * (-(-(SUBS + WIND_STAGES) // 8) * 8)
    f32 = jnp.float32
    dma = pltpu.SemaphoreType.DMA
    anywhere = pl.BlockSpec(memory_space=pl.ANY)
    vmem = pl.BlockSpec(memory_space=pltpu.VMEM)
    done, wind_new = pl.pallas_call(
        functools.partial(kernel, sizes),
        out_shape=(
            pltpu.VMEM((rows, species, width), f32),
            pltpu.VMEM(winds.shape, f32),
        ),
        in_specs=[pl.BlockSpec(memory_space=pltpu.HBM)] + [anywhere] * 6,
        out_specs=(vmem, vmem),
        scratch_shapes=[
            pltpu.VMEM((SUBS + 1, held, species, width), f32),
            pltpu.VMEM((2, wrows, width), f32),
            pltpu.VMEM((5, wrows, width), f32),
            pltpu.VMEM(linear.shape, f32),
            pltpu.VMEM((1, species), f32),
            pltpu.VMEM((2,) + left.shape, f32),
            pltpu.VMEM(((1 + 2 * pairs) * species, 2 * species), jnp.bfloat16),
            dma((rows,)),
            dma((4,)),
            pltpu.SMEM((1,), jnp.int32),
            dma,
            dma,
            dma((2, SUBS)),
            dma((2, SUBS)),
            dma((2,)),
            dma((2,)),
        ],
        compiler_params=pltpu.CompilerParams(collective_id=0, has_side_effects=True),
    )(active, tracers, winds, linear, loss.reshape(1, species), left, right)
    return pl.pallas_call(
        finish,
        out_shape=(
            jax.ShapeDtypeStruct(tracers.shape, f32),
            jax.ShapeDtypeStruct(winds.shape, f32),
        ),
        in_specs=[vmem, vmem],
        out_specs=(anywhere, anywhere),
        scratch_shapes=[dma((rows,)), dma],
    )(
        pltpu.with_memory_space_constraint(done, pltpu.VMEM),
        pltpu.with_memory_space_constraint(wind_new, pltpu.VMEM),
    )


def solution(mesh):
    sizes = tuple(mesh.shape[axis] for axis in AXES)
    banded = P(None, AXES, None)
    return jax.shard_map(
        functools.partial(on_device, sizes),
        mesh=mesh,
        in_specs=(banded, banded, P(), P(), P(), P(), P(AXES)),
        out_specs=(banded, banded),
        check_vma=False,
    )
```
